256 devices in a mesh: dp: 4 (over x), expert: 64 (over y, z, core).
Axes of the slice: x: 4, y: 4, z: 8, core: 2. Of those that a mesh axis runs over, the one named last changes fastest.
Arguments:
- tokens: bfloat16 [32768, 2048], P(('dp', 'expert')), may hold values from -6 to 6
- cotangent: bfloat16 [32768, 2048], P(('dp', 'expert')), may hold values from -1.5 to 1.5
- probs: bfloat16 [32768, 2], P(('dp', 'expert')), may hold values from 0.099609375 to 1
- expert_ids: int32 [32768, 2], P(('dp', 'expert')), may hold values from 0 to 63, all different within a row; in each aligned block of 128 rows (0 to 127, 128 to 255, ...) at most 8 rows name the same one
- holder: int32 [64], replicated, may hold values from 0 to 63, each once
- partner: int32 [64], replicated, may hold values from 0 to 63, as said below
- w_gate: bfloat16 [64, 2048, 768], P('expert', 'dp'), may hold values from -0.125 to 0.125
- w_up: bfloat16 [64, 2048, 768], P('expert', 'dp'), may hold values from -0.125 to 0.125
- w_down: bfloat16 [64, 768, 2048], P('expert', None, 'dp'), may hold values from -0.21875 to 0.21875
Outputs:
- grad_tokens: bfloat16 [32768, 2048], P(('dp', 'expert'))
- grad_probs: bfloat16 [32768, 2], P(('dp', 'expert'))
- grad_gate: bfloat16 [64, 2048, 768], P('expert', 'dp')
- grad_up: bfloat16 [64, 2048, 768], P('expert', 'dp')
- grad_down: bfloat16 [64, 768, 2048], P('expert', None, 'dp')
The draws below stay inside these ranges and needn't reach their ends.
Inputs may be any that keep to these rules, and one draw needn't show every extreme that they name: `expert_ids`: within each aligned block of 128 token rows (the rows of one device), no expert is named by more than 8 token-pick pairs, a bound that some block reaches; a row names 2 different experts. `holder`: every expert once. A perfect matching: partner[partner[j]] = j and partner[j] != j.
All inputs are finite; a program needn't handle non-finite values.
Results may differ from the reference program's by a relative error of at most 0.013.
Values may be sent and summed in bfloat16 or wider, within the bound.
A program may use at most 128 MiB of HBM per device.

```python
import math
import jax
import jax.numpy as jnp
import numpy as np
from jax import lax

D = 2048
FF = 768
TOPK = 2
TOK_DEV = 128
EXPERTS = 64
CAP = 8
TOKENS = 32768
N_DP = 4
N_EXPERT = 64


def draw_partner(key, part):
    order = jax.random.permutation(key, EXPERTS).astype(jnp.int32)
    firsts = order[0::2]
    seconds = order[1::2]
    result = jnp.zeros((EXPERTS,), jnp.int32).at[firsts].set(seconds).at[seconds].set(firsts)
    return result.astype(jnp.int32)


def block_levels(own_key, shape, pieces, low, high):
    level = 1.0
    for axis_at, shards_of in pieces:
        draws = jax.random.uniform(jax.random.fold_in(jax.random.fold_in(own_key, 6), axis_at), (shards_of,), jnp.float32, low / len(pieces), high / len(pieces))
        level = level * jnp.repeat(jnp.exp(draws), shape[axis_at] // shards_of).reshape((-1,) + (1,) * (len(shape) - 1 - axis_at))
    return level


def routed_block(own_key, own, number, rows, amount, top, bound, skew):
    ranking = jax.random.permutation(own_key, amount)
    packed, ordinary = portions_of(amount, rows * top, bound, skew, True), portions_of(amount, rows * top, bound, skew, False)
    places = jnp.arange(amount)

    def named(lengths, offset_by):
        used = int((lengths > 0).sum())
        fixed = max(1, used // 4)
        shifted = fixed + (places - fixed + offset_by * (used - fixed)) % max(1, amount - fixed)
        return jnp.zeros((amount,), jnp.int32).at[ranking[jnp.where(places < fixed, places, shifted)]].set(jnp.asarray(lengths, jnp.int32))

    lengths = jnp.where(number % 4 == 0, named(packed, number // 4), named(ordinary, number - number // 4 - 1))
    mixed = jax.random.permutation(jax.random.fold_in(own, 3), amount)
    source_of, sink = mixed[0:amount // 2 * 2:2], mixed[1:amount // 2 * 2:2]
    room = jnp.minimum(lengths[source_of] - 1, bound - lengths[sink]) // 2
    room = jnp.where((source_of == ranking[0]) | (sink == ranking[0]) | (lengths[sink] == 0), 0, jnp.maximum(room, 0))
    shifted = jax.random.randint(jax.random.fold_in(own, 4), (amount // 2,), 0, 1 << 20) % (room + 1)
    lengths = lengths.at[source_of].add(-shifted).at[sink].add(shifted)
    items = jnp.searchsorted(jnp.cumsum(lengths), jnp.arange(rows * top), side="right").astype(jnp.int32)
    listing = items.reshape(top, rows).T
    listing = listing[jax.random.permutation(jax.random.fold_in(own, 1), rows)]
    offset_by = jax.random.randint(jax.random.fold_in(own, 2), (rows, 1), 0, top)
    return jnp.take_along_axis(listing, (jnp.arange(top)[None, :] + offset_by) % top, axis=1)


def portions_of(number_of, total, reach, lean, full):
    loads = [(1 << 20) // math.isqrt(standing ** lean) + 1 for standing in range(1, number_of + 1)]
    largest = reach if full else min(reach, max(-(-total // number_of), total * loads[0] // sum(loads)))
    least = 1 if total - largest >= number_of - 1 else 0
    counts, spare = [largest] + [least] * (number_of - 1), total - largest - least * (number_of - 1)
    while spare > 0:
        free = [i for i in range(1, number_of) if counts[i] < largest] or [i for i in range(1, number_of) if counts[i] < reach]
        whole, left = sum([loads[i] for i in free]), spare
        for i in free:
            more = min(reach - counts[i], max(1, left * loads[i] // whole), spare)
            counts[i] = counts[i] + more
            spare = spare - more
    return np.array(counts)


def centred(own_key, dims, deviation, reach, split=(), kind=jnp.bfloat16):
    gain = block_levels(own_key, dims, split, -0.22, 0.18) if split else 1.0
    values = jax.random.normal(own_key, dims, jnp.float32) * deviation * gain
    return jnp.minimum(jnp.maximum(values, -reach), reach).astype(kind)


def setup_inputs(seed: int = 0) -> dict:
    splits = jax.random.split(jax.random.key(seed), 10)
    tokens = centred(splits[0], (TOKENS, D), 1.0, 6.0, ((0, 256),))
    cotangent = centred(splits[1], (TOKENS, D), 0.25, 1.5, ((0, 256),))
    probs = jnp.clip(jnp.exp(math.log(1.0) - 2.306499 * jax.random.uniform(splits[2], (TOKENS, TOPK), jnp.float32) ** block_levels(splits[2], (TOKENS, TOPK), ((0, 256),), -0.2, 0.2)), 0.099609375, 1.0).astype(jnp.bfloat16)
    expert_ids_keys = jax.random.split(jax.random.fold_in(splits[3], 1), TOKENS // TOK_DEV)
    expert_ids_turns = jax.random.permutation(jax.random.fold_in(splits[3], 3), TOKENS // TOK_DEV)
    expert_ids = jax.vmap(lambda own, number: routed_block(jax.random.fold_in(splits[3], 2), own, number, TOK_DEV, EXPERTS, TOPK, CAP, 2))(expert_ids_keys, expert_ids_turns).reshape((TOKENS, TOPK))
    holder = jax.random.permutation(splits[4], EXPERTS).astype(jnp.int32)
    partner = draw_partner(jax.random.fold_in(splits[9], 71), 0)
    w_gate = centred(splits[6], (EXPERTS, D, FF), D ** -0.5, 0.125, ((0, 64), (1, 4)))
    w_up = centred(splits[7], (EXPERTS, D, FF), D ** -0.5, 0.125, ((0, 64), (1, 4)))
    w_down = centred(splits[8], (EXPERTS, FF, D), FF ** -0.5, 0.21875, ((0, 64), (2, 4)))
    return dict(tokens=tokens, cotangent=cotangent, probs=probs, expert_ids=expert_ids, holder=holder, partner=partner, w_gate=w_gate, w_up=w_up, w_down=w_down)


def expert_pass(rows_x, rows_dy, rows_p, gate_w, up_w, down_w):
    x_wide = rows_x.astype(jnp.float32)
    gate_pre = jnp.dot(x_wide, gate_w.astype(jnp.float32))
    up_pre = jnp.dot(x_wide, up_w.astype(jnp.float32))
    gate_sig = jax.nn.sigmoid(gate_pre)
    hidden = (gate_pre * gate_sig * up_pre).astype(jnp.bfloat16)
    expert_out = jnp.dot(hidden.astype(jnp.float32), down_w.astype(jnp.float32)).astype(jnp.bfloat16)
    scaled = (rows_p.astype(jnp.float32)[:, None] * rows_dy.astype(jnp.float32)).astype(jnp.bfloat16)
    d_hidden = jnp.dot(scaled.astype(jnp.float32), down_w.astype(jnp.float32).T)
    d_gate = (d_hidden * up_pre * gate_sig * (1.0 + gate_pre * (1.0 - gate_sig))).astype(jnp.bfloat16)
    d_up = (d_hidden * gate_pre * gate_sig).astype(jnp.bfloat16)
    pair_grad = (jnp.dot(d_gate.astype(jnp.float32), gate_w.astype(jnp.float32).T)
                 + jnp.dot(d_up.astype(jnp.float32), up_w.astype(jnp.float32).T)).astype(jnp.bfloat16)
    score = jnp.sum(rows_dy.astype(jnp.float32) * expert_out.astype(jnp.float32), axis=1)
    return hidden, scaled, d_gate, d_up, pair_grad, score


def group_sum(left, right, part):
    total = jnp.zeros((left.shape[1], right.shape[1]), jnp.float32)
    for group in range(N_DP):
        lower = group * part
        piece = jnp.dot(left[lower:lower + part].astype(jnp.float32).T, right[lower:lower + part].astype(jnp.float32))
        rounded = lax.optimization_barrier(piece.astype(jnp.bfloat16))
        total = total + rounded.astype(jnp.float32)
    return total.astype(jnp.bfloat16)


def reference(tokens, cotangent, probs, expert_ids, holder, partner, w_gate, w_up, w_down):
    groups = N_DP * N_EXPERT
    pair_count = TOK_DEV * TOPK
    flat_ids = expert_ids.reshape(groups, pair_count)
    numbers = jnp.arange(EXPERTS, dtype=jnp.int32)
    onehot = (flat_ids[:, :, None] == numbers[None, None, :]).astype(jnp.int32)
    earlier = jnp.cumsum(onehot, axis=1) - onehot
    slot_index = jnp.sum(earlier * onehot, axis=2).astype(jnp.int32)
    group_ids = jnp.arange(groups, dtype=jnp.int32)[:, None]
    position = ((flat_ids * groups + group_ids) * CAP + slot_index).astype(jnp.int32)
    pair_ids = jnp.arange(TOKENS * TOPK, dtype=jnp.int32)
    empty_pair = TOKENS * TOPK
    pair_table = jnp.full((EXPERTS * groups * CAP,), empty_pair, jnp.int32).at[position.reshape(-1)].set(pair_ids)
    pair_table = pair_table.reshape(EXPERTS, groups * CAP)
    token_table = (pair_table // TOPK).astype(jnp.int32)
    zero_row = jnp.zeros((1, D), jnp.bfloat16)
    x_ext = jnp.concatenate([tokens, zero_row], axis=0)
    dy_ext = jnp.concatenate([cotangent, zero_row], axis=0)
    p_ext = jnp.concatenate([probs.reshape(-1), jnp.zeros((1,), jnp.bfloat16)], axis=0)
    home_slot = jnp.argsort(holder).astype(jnp.int32)
    part = N_EXPERT * CAP

    def one_expert(carry, expert):
        grad_acc, score_acc = carry
        pair_rows = pair_table[expert]
        token_rows = token_table[expert]
        rows_x = x_ext[token_rows]
        rows_dy = dy_ext[token_rows]
        rows_p = p_ext[pair_rows]
        where = home_slot[expert]
        hidden, scaled, d_gate, d_up, pair_grad, score = expert_pass(
            rows_x, rows_dy, rows_p, w_gate[where], w_up[where], w_down[where])
        grad_acc = grad_acc.at[token_rows].add(pair_grad.astype(jnp.float32))
        score_acc = score_acc.at[pair_rows].set(score)
        grads = (group_sum(rows_x, d_gate, part), group_sum(rows_x, d_up, part), group_sum(hidden, scaled, part))
        return (grad_acc, score_acc), grads

    start = (jnp.zeros((TOKENS + 1, D), jnp.float32), jnp.zeros((TOKENS * TOPK + 1,), jnp.float32))
    (grad_acc, score_acc), (all_gate, all_up, all_down) = lax.scan(one_expert, start, numbers)
    grad_tokens = grad_acc[:TOKENS].astype(jnp.bfloat16)
    grad_probs = score_acc[:TOKENS * TOPK].reshape(TOKENS, TOPK).astype(jnp.bfloat16)
    after = holder[partner]
    return grad_tokens, grad_probs, all_gate[after], all_up[after], all_down[after]
```

```python
import jax
import jax.numpy as jnp
from jax import lax
from jax.sharding import PartitionSpec as P

RIGHT = [(0, 1), (1, 2), (2, 3), (3, 0)]
LEFT = [(1, 0), (2, 1), (3, 2), (0, 3)]


def dot_f32(left, right, dims):
    return lax.dot_general(left, right, (dims, ((), ())), preferred_element_type=jnp.float32)


def send_near(tile):
    return lax.ppermute(tile, "dp", RIGHT), lax.ppermute(tile, "dp", LEFT)


def send_far(near):
    from_left, from_right = near
    half = from_left.shape[0] // 2
    top = lax.ppermute(from_left[:half], "dp", RIGHT)
    low = lax.ppermute(from_right[half:], "dp", LEFT)
    return jnp.concatenate([top, low], axis=0)


def scatter_far(opposite):
    half = opposite.shape[0] // 2
    return lax.ppermute(opposite[:half], "dp", RIGHT), lax.ppermute(opposite[half:], "dp", LEFT)


def scatter_near(right, left, top, low):
    half = right.shape[0] // 2
    add = lambda a, b: (a.astype(jnp.float32) + b.astype(jnp.float32)).astype(jnp.bfloat16)
    send_right = jnp.concatenate([add(right[:half], top), right[half:]], axis=0)
    send_left = jnp.concatenate([left[:half], add(left[half:], low)], axis=0)
    return lax.ppermute(send_right, "dp", RIGHT), lax.ppermute(send_left, "dp", LEFT)


def total3(own, from_left, from_right):
    f32 = jnp.float32
    return (own.astype(f32) + from_left.astype(f32) + from_right.astype(f32)).astype(jnp.bfloat16)


def exchange(rows):
    return lax.all_to_all(rows, "expert", split_axis=0, concat_axis=0, tiled=True)


def shards(tokens, cotangent, probs, expert_ids, holder, partner, w_gate, w_up, w_down):
    experts = holder.shape[0]
    tok_rows, picks = expert_ids.shape
    pair_count = tok_rows * picks
    capacity = 2 * pair_count // experts
    slots = experts * capacity
    width = tokens.shape[1]
    tile = w_gate.shape[1]
    shift = lax.axis_index("dp") * tile
    f32, bf16 = jnp.float32, jnp.bfloat16

    near_gate, near_up, near_down = send_near(w_gate[0]), send_near(w_up[0]), send_near(w_down[0])

    numbers = jnp.arange(experts, dtype=jnp.int32)
    home = jnp.sum((holder[None, :] == numbers[:, None]).astype(jnp.int32) * numbers[None, :], axis=1)
    flat = expert_ids.reshape(pair_count)
    order = jnp.arange(pair_count, dtype=jnp.int32)
    same = (flat[:, None] == flat[None, :]) & (order[None, :] < order[:, None])
    slot = jnp.sum(same.astype(jnp.int32), axis=1)
    dest = jnp.sum((flat[:, None] == numbers[None, :]).astype(jnp.int32) * home[None, :], axis=1)
    pair_row = (dest * capacity + slot).reshape(tok_rows, picks)
    row_ids = jnp.arange(slots, dtype=jnp.int32)
    first = row_ids[:, None] == pair_row[:, 0][None, :]
    second = row_ids[:, None] == pair_row[:, 1][None, :]
    pick = (first | second).astype(bf16)
    zero = jnp.zeros((), bf16)
    weighted = jnp.where(first, probs[:, 0][None, :], jnp.where(second, probs[:, 1][None, :], zero))

    def rolled(a):
        return lax.dynamic_slice(jnp.concatenate([a, a], axis=1), (0, shift), a.shape)

    send_x = dot_f32(pick, rolled(tokens), ((1,), (0,))).astype(bf16)
    recv_x = exchange(send_x.reshape(experts, capacity, width)).reshape(slots, width)
    send_s = dot_f32(weighted, rolled(cotangent), ((1,), (0,))).astype(bf16)
    send_s, near_gate, near_up, near_down = lax.optimization_barrier((send_s, near_gate, near_up, near_down))
    recv_s = exchange(send_s.reshape(experts, capacity, width)).reshape(slots, width)
    far_gate, far_up, far_down = send_far(near_gate), send_far(near_up), send_far(near_down)
    gate_w = jnp.concatenate([w_gate[0], near_gate[1], far_gate, near_gate[0]], axis=0)
    up_w = jnp.concatenate([w_up[0], near_up[1], far_up, near_up[0]], axis=0)
    down_w = jnp.concatenate([w_down[0], near_down[1], far_down, near_down[0]], axis=1)

    gate_pre = dot_f32(recv_x, gate_w, ((1,), (0,)))
    up_pre = dot_f32(recv_x, up_w, ((1,), (0,)))
    recv_s, gate_pre, up_pre, down_w = lax.optimization_barrier((recv_s, gate_pre, up_pre, down_w))
    d_hidden = dot_f32(recv_s, down_w, ((1,), (1,)))
    sig = jax.nn.sigmoid(gate_pre)
    hidden = (gate_pre * sig * up_pre).astype(bf16)
    d_gate = (d_hidden * up_pre * sig * (1.0 + gate_pre * (1.0 - sig))).astype(bf16)
    d_up = (d_hidden * gate_pre * sig).astype(bf16)
    score = jnp.sum(hidden.astype(f32) * d_hidden, axis=1, keepdims=True)
    high = score.astype(bf16)
    low = (score - high.astype(f32)).astype(bf16)
    lanes = jnp.arange(128, dtype=jnp.int32)[None, :]
    extra = jnp.where(lanes == 0, high, jnp.where(lanes == 1, low, zero))
    pair_grad = (dot_f32(d_gate, gate_w, ((1,), (1,))) + dot_f32(d_up, up_w, ((1,), (1,)))).astype(bf16)
    send_back = jnp.concatenate([pair_grad, extra], axis=1)
    send_back, hidden, d_gate, d_up = lax.optimization_barrier((send_back, hidden, d_gate, d_up))
    wide = width + 128
    back = exchange(send_back.reshape(experts, capacity, wide)).reshape(slots, wide)

    def blocks(left, right):
        full = dot_f32(left, right, ((0,), (0,))).astype(bf16)
        return [full[i * tile : (i + 1) * tile] for i in range(4)]

    def reduce_dp(own, right, opposite, left):
        top, low = scatter_far(opposite)
        return total3(own, *scatter_near(right, left, top, low))

    hid = w_gate.shape[2]
    rows = tile // experts
    sum_down = reduce_dp(*blocks(recv_s, hidden)).reshape(experts, rows, hid)
    sum_gate = reduce_dp(*blocks(recv_x, d_gate)).reshape(experts, rows, hid)
    sum_up = reduce_dp(*blocks(recv_x, d_up)).reshape(experts, rows, hid)
    sum_down, back = lax.optimization_barrier((sum_down, back))
    spread_down = exchange(sum_down)
    sum_gate, sum_up, spread_down = lax.optimization_barrier((sum_gate, sum_up, spread_down))
    spread_rest = exchange(jnp.concatenate([sum_gate, sum_up], axis=1))
    spread = jnp.concatenate([spread_rest, spread_down], axis=1)
    traded = exchange(jnp.take(spread, partner, axis=0, mode="clip"))
    grad_gate, grad_up, grad_down = [
        traded[:, i * rows : (i + 1) * rows].reshape(tile, hid) for i in range(3)
    ]

    mixed = dot_f32(pick.T, back[:, :width], ((1,), (0,))).astype(bf16)
    grad_tokens = lax.dynamic_slice(
        jnp.concatenate([mixed, mixed], axis=1), (0, (width - shift) % width), mixed.shape
    )
    picked = [
        jnp.sum(dot_f32(hit.astype(bf16), back[:, width:], ((0,), (0,))), axis=1) for hit in (first, second)
    ]
    grad_probs = (jnp.stack(picked, axis=1) / probs.astype(f32)).astype(bf16)
    return grad_tokens, grad_probs, grad_gate[None], grad_up[None], grad_down.T[None]


def solution(mesh):
    rows = P(("dp", "expert"), None)
    wide, tall = P("expert", "dp", None), P("expert", None, "dp")
    return jax.shard_map(
        shards,
        mesh=mesh,
        in_specs=(rows, rows, rows, rows, P(), P(), wide, wide, tall),
        out_specs=(rows, rows, wide, wide, tall),
        check_vma=False,
    )
```

```python
import functools

import jax
import jax.numpy as jnp
from jax import lax
from jax.experimental import pallas as pl
from jax.experimental.pallas import tpu as pltpu
from jax.sharding import PartitionSpec as P

RIGHT = [(0, 1), (1, 2), (2, 3), (3, 0)]
LEFT = [(1, 0), (2, 1), (3, 2), (0, 3)]


def dot_f32(left, right, dims):
    return lax.dot_general(left, right, (dims, ((), ())), preferred_element_type=jnp.float32)


def send_near(tile):
    return lax.ppermute(tile, "dp", RIGHT), lax.ppermute(tile, "dp", LEFT)


def send_far(near):
    from_left, from_right = near
    half = from_left.shape[0] // 2
    top = lax.ppermute(from_left[:half], "dp", RIGHT)
    low = lax.ppermute(from_right[half:], "dp", LEFT)
    return jnp.concatenate([top, low], axis=0)


def exchange(rows):
    return lax.all_to_all(rows, "expert", split_axis=0, concat_axis=0, tiled=True)


def finish_kernel(
    n, partner, back, hits, part_down, part_gate, part_up,
    tok_out, score_out, down_out, gate_out, up_out,
    back_in, far_in, near_out, near_in, summed, spread_a, spread_b, spread_c, turned,
    back_send, back_recv, own_sem, far_send, far_recv, near_send, near_recv,
    spread_send, spread_recv, final_send, final_recv,
):
    me = lax.axis_index("expert")
    dp = lax.axis_index("dp")
    right, left = {"dp": lax.rem(dp + 1, 4)}, {"dp": lax.rem(dp + 3, 4)}
    parts = (part_down, part_gate, part_up)
    outs = (down_out, gate_out, up_out)
    spread = (spread_a, spread_b, spread_c)
    half = part_down.shape[1] // 2
    f32, bf16 = jnp.float32, jnp.bfloat16

    def peer(k):
        return lax.rem(me + k, n)

    barrier = pltpu.get_barrier_semaphore()

    def greet(k, carry):
        pl.semaphore_signal(barrier, inc=1, device_id={"expert": peer(k)}, device_id_type=pl.DeviceIdType.MESH)
        return carry

    lax.fori_loop(1, n, greet, 0)
    for side in (right, left):
        pl.semaphore_signal(barrier, inc=1, device_id=side, device_id_type=pl.DeviceIdType.MESH)
    pl.semaphore_wait(barrier, n + 1)

    def remote(src, dst, send, recv, device):
        return pltpu.make_async_remote_copy(
            src_ref=src, dst_ref=dst, send_sem=send, recv_sem=recv,
            device_id=device, device_id_type=pl.DeviceIdType.MESH,
        )

    def far_copies(a):
        opposite = parts[a].at[2]
        return [
            remote(opposite.at[pl.ds(d * half, half)], far_in.at[a, d], far_send.at[a, d], far_recv.at[a, d], side)
            for d, side in enumerate((right, left))
        ]

    def near_copies(a):
        return [
            remote(near_out.at[a, d], near_in.at[a, d], near_send.at[a, d], near_recv.at[a, d], side)
            for d, side in enumerate((right, left))
        ]

    def all_to_all(src, dst, send, recv, own):
        keep = pltpu.make_async_copy(src.at[me], dst.at[me], own)

        def start(k, carry):
            to = peer(k)
            remote(src.at[to], dst.at[me], send, recv, {"expert": to}).start()
            return carry

        lax.fori_loop(1, n, start, 0)
        keep.start()
        others = pl.ds(0, n - 1)
        whole = remote(src.at[others], dst.at[others], send, recv, {"expert": peer(1)})
        return keep, whole

    def arrived(pair):
        pair[0].wait()
        pair[1].wait_recv()

    rows = 64

    def add_far(a):
        for copy in far_copies(a):
            copy.wait_recv()

        def body(i, carry):
            top = pl.ds(pl.multiple_of(i * rows, rows), rows)
            low = pl.ds(pl.multiple_of(half + i * rows, rows), rows)
            near_out[a, 0, top] = (parts[a][1, top].astype(f32) + far_in[a, 0, top].astype(f32)).astype(bf16)
            near_out[a, 0, low] = parts[a][1, low]
            near_out[a, 1, top] = parts[a][3, top]
            near_out[a, 1, low] = (parts[a][3, low].astype(f32) + far_in[a, 1, top].astype(f32)).astype(bf16)
            return carry

        lax.fori_loop(0, half // rows, body, 0)
        for copy in near_copies(a):
            copy.start()

    def add_near(a):
        for copy in near_copies(a):
            copy.wait_recv()
        piece = summed.shape[2]
        per = rows // piece

        def body(i, carry):
            at = pl.ds(pl.multiple_of(i * rows, rows), rows)
            total = parts[a][0, at].astype(f32) + near_in[a, 0, at].astype(f32) + near_in[a, 1, at].astype(f32)
            summed[a, pl.ds(i * per, per)] = total.astype(bf16).reshape(per, piece, total.shape[1])
            return carry

        lax.fori_loop(0, 2 * half // rows, body, 0)
        return all_to_all(summed.at[a], spread[a], spread_send.at[a], spread_recv.at[a], own_sem.at[1 + a])

    def turn(a, pair):
        arrived(pair)

        def body(j, carry):
            turned[a, j] = spread[a][partner[j]]
            return carry

        lax.fori_loop(0, n, body, 0)
        return all_to_all(turned.at[a], outs[a], final_send.at[a], final_recv.at[a], own_sem.at[4 + a])

    for copy in far_copies(0) + far_copies(1):
        copy.start()
    back_pair = all_to_all(back, back_in, back_send, back_recv, own_sem.at[0])
    add_far(0)
    for copy in far_copies(2):
        copy.start()
    add_far(1)
    add_far(2)
    first = [add_near(a) for a in range(3)]

    arrived(back_pair)
    wide = back_in.shape[2]
    width = tok_out.shape[1]
    count = tok_out.shape[0]
    block = width // 4
    rows_in = back_in[...].reshape(n * back_in.shape[1], wide)
    for i in range(4):
        both = jnp.dot(hits[...], rows_in[:, i * block : (i + 1) * block], preferred_element_type=f32)
        at = pl.multiple_of(lax.rem(dp + i, 4) * block, block)
        tok_out[:, pl.ds(at, block)] = (both[:count] + both[count:]).astype(bf16)
    score_out[...] = jnp.dot(hits[...], rows_in[:, width:], preferred_element_type=f32)

    second = [turn(a, first[a]) for a in range(3)]
    for pair in second:
        arrived(pair)
    for a in range(3):
        for copy in far_copies(a) + near_copies(a):
            copy.wait_send()
    for pair in [back_pair] + first + second:
        pair[1].wait_send()


def finish(partner, back, hits, parts, width):
    n, cap, wide = back.shape
    count = hits.shape[0] // 2
    tile, hid = parts[0].shape[1:]
    piece = tile // n
    bf16 = jnp.bfloat16
    vmem, dma = pl.BlockSpec(memory_space=pltpu.VMEM), pltpu.SemaphoreType.DMA
    grad = jax.ShapeDtypeStruct((n, piece, hid), bf16)
    return pl.pallas_call(
        functools.partial(finish_kernel, n),
        out_shape=(
            jax.ShapeDtypeStruct((count, width), bf16),
            jax.ShapeDtypeStruct((2 * count, wide - width), jnp.float32),
            grad, grad, grad,
        ),
        in_specs=[pl.BlockSpec(memory_space=pltpu.SMEM)] + [vmem] * 5,
        out_specs=[vmem] * 5,
        scratch_shapes=[
            pltpu.VMEM((n, cap, wide), bf16),
            pltpu.VMEM((3, 2, tile // 2, hid), bf16),
            pltpu.VMEM((3, 2, tile, hid), bf16),
            pltpu.VMEM((3, 2, tile, hid), bf16),
            pltpu.VMEM((3, n, piece, hid), bf16),
            pltpu.VMEM((n, piece, hid), bf16),
            pltpu.VMEM((n, piece, hid), bf16),
            pltpu.VMEM((n, piece, hid), bf16),
            pltpu.VMEM((3, n, piece, hid), bf16),
            dma, dma, dma((7,)), dma((3, 2)), dma((3, 2)), dma((3, 2)), dma((3, 2)),
            dma((3,)), dma((3,)), dma((3,)), dma((3,)),
        ],
        compiler_params=pltpu.CompilerParams(
            collective_id=0, has_side_effects=True, vmem_limit_bytes=60 * 1024 * 1024
        ),
    )(partner, back, hits, *parts)


def shards(tokens, cotangent, probs, expert_ids, holder, partner, w_gate, w_up, w_down):
    experts = holder.shape[0]
    tok_rows, picks = expert_ids.shape
    pair_count = tok_rows * picks
    capacity = 2 * pair_count // experts
    slots = experts * capacity
    width = tokens.shape[1]
    tile = w_gate.shape[1]
    shift = lax.axis_index("dp") * tile
    f32, bf16 = jnp.float32, jnp.bfloat16

    down_t = w_down[0].T
    near_gate, near_up, near_down = send_near(w_gate[0]), send_near(w_up[0]), send_near(down_t)

    numbers = jnp.arange(experts, dtype=jnp.int32)
    home = jnp.sum((holder[None, :] == numbers[:, None]).astype(jnp.int32) * numbers[None, :], axis=1)
    flat = expert_ids.reshape(pair_count)
    order = jnp.arange(pair_count, dtype=jnp.int32)
    same = (flat[:, None] == flat[None, :]) & (order[None, :] < order[:, None])
    slot = jnp.sum(same.astype(jnp.int32), axis=1)
    dest = jnp.sum((flat[:, None] == numbers[None, :]).astype(jnp.int32) * home[None, :], axis=1)
    pair_row = (dest * capacity + slot).reshape(tok_rows, picks)
    row_ids = jnp.arange(slots, dtype=jnp.int32)
    first = row_ids[:, None] == pair_row[:, 0][None, :]
    second = row_ids[:, None] == pair_row[:, 1][None, :]
    pick = (first | second).astype(bf16)
    zero = jnp.zeros((), bf16)
    weighted = jnp.where(first, probs[:, 0][None, :], jnp.where(second, probs[:, 1][None, :], zero))

    def rolled(a):
        return lax.dynamic_slice(jnp.concatenate([a, a], axis=1), (0, shift), a.shape)

    send_x = dot_f32(pick, rolled(tokens), ((1,), (0,))).astype(bf16)
    recv_x = exchange(send_x.reshape(experts, capacity, width)).reshape(slots, width)
    send_s = dot_f32(weighted, rolled(cotangent), ((1,), (0,))).astype(bf16)
    send_s, near_gate, near_up, near_down = lax.optimization_barrier((send_s, near_gate, near_up, near_down))
    recv_s = exchange(send_s.reshape(experts, capacity, width)).reshape(slots, width)
    far_gate, far_up, far_down = send_far(near_gate), send_far(near_up), send_far(near_down)
    gate_w = jnp.concatenate([w_gate[0], near_gate[1], far_gate, near_gate[0]], axis=0)
    up_w = jnp.concatenate([w_up[0], near_up[1], far_up, near_up[0]], axis=0)
    down_w = jnp.concatenate([down_t, near_down[1], far_down, near_down[0]], axis=0)

    gate_pre = dot_f32(recv_x, gate_w, ((1,), (0,)))
    up_pre = dot_f32(recv_x, up_w, ((1,), (0,)))
    recv_s, gate_pre, up_pre, down_w = lax.optimization_barrier((recv_s, gate_pre, up_pre, down_w))
    d_hidden = dot_f32(recv_s, down_w, ((1,), (0,)))
    sig = jax.nn.sigmoid(gate_pre)
    hidden = (gate_pre * sig * up_pre).astype(bf16)
    d_gate = (d_hidden * up_pre * sig * (1.0 + gate_pre * (1.0 - sig))).astype(bf16)
    d_up = (d_hidden * gate_pre * sig).astype(bf16)
    score = jnp.sum(hidden.astype(f32) * d_hidden, axis=1, keepdims=True)
    high = score.astype(bf16)
    low = (score - high.astype(f32)).astype(bf16)
    lanes = jnp.arange(128, dtype=jnp.int32)[None, :]
    extra = jnp.where(lanes == 0, high, jnp.where(lanes == 1, low, zero))
    pair_grad = (dot_f32(d_gate, gate_w, ((1,), (1,))) + dot_f32(d_up, up_w, ((1,), (1,)))).astype(bf16)
    send_back = jnp.concatenate([pair_grad, extra], axis=1)
    hid = w_gate.shape[2]

    def blocks(left, right):
        return dot_f32(left, right, ((0,), (0,))).astype(bf16).reshape(4, tile, hid)

    parts = (blocks(recv_s, hidden), blocks(recv_x, d_gate), blocks(recv_x, d_up))
    hits = jnp.concatenate([first.T, second.T], axis=0).astype(bf16)
    grad_tokens, scores, grad_down, grad_gate, grad_up = finish(
        partner, send_back.reshape(experts, capacity, width + 128), hits, parts, width
    )
    picked = (scores[:, 0] + scores[:, 1]).reshape(picks, tok_rows).T
    grad_probs = (picked / probs.astype(f32)).astype(bf16)
    grad_gate, grad_up, grad_down = [a.reshape(tile, hid) for a in (grad_gate, grad_up, grad_down)]
    return grad_tokens, grad_probs, grad_gate[None], grad_up[None], grad_down.T[None]


def solution(mesh):
    rows = P(("dp", "expert"), None)
    wide, tall = P("expert", "dp", None), P("expert", None, "dp")
    return jax.shard_map(
        shards,
        mesh=mesh,
        in_specs=(rows, rows, rows, rows, P(), P(), wide, wide, tall),
        out_specs=(rows, rows, wide, wide, tall),
        check_vma=False,
    )
```
